32 devices in a mesh: gx: 8 (over y, x, core), row: 4 (over z).
Axes of the slice: x: 2, y: 2, z: 4, core: 2. Of those that a mesh axis runs over, the one named last changes fastest.
Arguments:
- amplitudes: float32 [128, 4096], P('gx', 'row'), may hold values from -6 to 6
- integrals: float32 [4096, 16384], P('row', 'gx'), may hold values from -0.1875 to 0.1875
- cd_irrep: int32 [32], P('row'), may hold values from 0 to 7
- ab_irrep: int32 [128], P('gx'), may hold values from 0 to 7
- allowed: int32 [8, 8], replicated, may hold values 0 or 1
- pair_occ: int32 [128, 2], P(('gx', 'row')), may hold values from 0 to 99
- occ_energy: float32 [100], replicated, may hold values from -1 to -0.25
- ab_energy: float32 [16384], replicated, may hold values from 1 to 4
Outputs:
- residual: float32 [128, 16384], P(('gx', 'row'))
- update: float32 [128, 16384], P(('gx', 'row'))
The draws below stay inside these ranges and needn't reach their ends.
All inputs are finite; a program needn't handle non-finite values.
Results may differ from the reference program's by a relative error of at most 0.000071.
Values sent between devices are 32-bit elements; how exact they have to be, the bound alone decides.
A program may use at most 128 MiB of HBM per device.

```python
import jax
import jax.numpy as jnp
from jax import lax

C = 4096
BLK = 128
NIRR = 8
NOCC = 100
AB_DEV = 2048
P_SIZE = 128
A = 16384
NCB = 32
NAB = 128
N_GX = 8


def set_ends(entries, stream_key, least, high):
    longest = entries.shape.index(max(entries.shape))
    spots = []
    for shift in (0, 1):
        where = [jax.random.randint(jax.random.fold_in(stream_key, axis), (), 0, length) for axis, length in enumerate(entries.shape)]
        where[longest] = (where[longest] + shift) % entries.shape[longest]
        spots.append(tuple(where))
    return entries.at[spots[0]].set(least).at[spots[1]].set(high)


def block_levels(own_key, dims, shards, least, high):
    loudness = 1.0
    for axis_at, blocks in shards:
        draws = jax.random.uniform(jax.random.fold_in(jax.random.fold_in(own_key, 6), axis_at), (blocks,), jnp.float32, least / len(shards), high / len(shards))
        loudness = loudness * jnp.repeat(jnp.exp(draws), dims[axis_at] // blocks).reshape((-1,) + (1,) * (len(dims) - 1 - axis_at))
    return loudness


def centred(rng, dims, scale, limit, pieces=(), kind=jnp.bfloat16):
    entries = scale * jax.random.normal(rng, dims, jnp.float32)
    if pieces:
        entries = entries * block_levels(rng, dims, pieces, -0.22, 0.18)
    return jnp.clip(entries, -limit, limit).astype(kind)


def setup_inputs(seed: int = 0) -> dict:
    key_list = jax.random.split(jax.random.key(seed), 9)
    return {
        "amplitudes": centred(key_list[0], (P_SIZE, C), 1.0, 6.0, ((0, 8), (1, 4)), jnp.float32),
        "integrals": centred(key_list[1], (C, A), (C // 4) ** -0.5, 0.1875, ((0, 4), (1, 8)), jnp.float32),
        "cd_irrep": set_ends(jax.random.randint(key_list[2], (NCB,), 0, NIRR), jax.random.fold_in(key_list[2], 1), 0, NIRR - 1).astype(jnp.int32),
        "ab_irrep": set_ends(jax.random.randint(key_list[3], (NAB,), 0, NIRR), jax.random.fold_in(key_list[3], 1), 0, NIRR - 1).astype(jnp.int32),
        "allowed": set_ends((jax.random.randint(key_list[4], (NIRR, NIRR), 0, 4) < 1).astype(jnp.int32), jax.random.fold_in(key_list[4], 1), 0, 1),
        "pair_occ": set_ends(jax.random.randint(key_list[5], (P_SIZE, 2), 0, NOCC), jax.random.fold_in(key_list[5], 1), 0, NOCC - 1).astype(jnp.int32),
        "occ_energy": jnp.clip(jax.random.uniform(key_list[6], (NOCC,), jnp.float32, -1.0, -0.25), -1.0, -0.25),
        "ab_energy": jnp.clip(jax.random.uniform(key_list[7], (A,), jnp.float32, 1.0, 4.0), 1.0, 4.0),
    }


def reference(amplitudes, integrals, cd_irrep, ab_irrep, allowed, pair_occ, occ_energy, ab_energy):
    block_mask = allowed[cd_irrep[:, None], ab_irrep[None, :]].astype(jnp.float32)
    ab_blocks = AB_DEV // BLK

    def one_slab(index):
        columns = lax.dynamic_slice_in_dim(integrals, index * AB_DEV, AB_DEV, 1)
        mask_part = lax.dynamic_slice_in_dim(block_mask, index * ab_blocks, ab_blocks, 1)
        effective = (columns.reshape(NCB, BLK, ab_blocks, BLK) * mask_part[:, None, :, None]).reshape(C, AB_DEV)
        return jnp.dot(amplitudes, effective, precision=lax.Precision.HIGHEST, preferred_element_type=jnp.float32)

    slabs = lax.map(one_slab, jnp.arange(N_GX, dtype=jnp.int32))
    residual = slabs.transpose(1, 0, 2).reshape(P_SIZE, A)
    pair_energy = occ_energy[pair_occ[:, 0]] + occ_energy[pair_occ[:, 1]]
    update = residual / (ab_energy[None, :] - pair_energy[:, None])
    return residual, update
```

```python
import functools

import jax
import jax.numpy as jnp
from jax import lax
from jax.experimental import pallas as pl
from jax.experimental.pallas import tpu as pltpu
from jax.sharding import PartitionSpec as P

BLK = 128
MESH = pl.DeviceIdType.MESH
VMEM_BUDGET = 48 * 2**20
VMEM_GRANT = 67043328
LAGS = (11, 5)


def plain_body(amplitudes, integrals, cd_irrep, ab_irrep, allowed, pair_occ, occ_energy, ab_energy):
    irrep_labels = jnp.arange(allowed.shape[0], dtype=jnp.int32)
    cd_onehot = (cd_irrep[:, None] == irrep_labels[None, :]).astype(jnp.float32)
    ab_onehot = (ab_irrep[:, None] == irrep_labels[None, :]).astype(jnp.float32)
    irrep_table = allowed.astype(jnp.float32)
    block_mask = jnp.dot(
        jnp.dot(cd_onehot, irrep_table, precision=lax.Precision.HIGHEST),
        ab_onehot.T,
        precision=lax.Precision.HIGHEST,
    )
    cd_rows, ab_cols = integrals.shape
    effective = (
        integrals.reshape(cd_rows // BLK, BLK, ab_cols // BLK, BLK) * block_mask[:, None, :, None]
    ).reshape(cd_rows, ab_cols)
    partial_value = jnp.dot(
        lax.all_gather(amplitudes, "gx", axis=0, tiled=True),
        effective,
        precision=lax.Precision.HIGHEST,
        preferred_element_type=jnp.float32,
    )
    arrived = lax.all_to_all(partial_value, "gx", split_axis=0, concat_axis=1, tiled=True)
    residual = lax.psum_scatter(arrived, "row", scatter_dimension=0, tiled=True)
    occ_labels = jnp.arange(occ_energy.shape[0], dtype=jnp.int32)
    pair_onehot = (pair_occ[:, :, None] == occ_labels[None, None, :]).astype(jnp.float32)
    pair_energy = jnp.sum(pair_onehot * occ_energy[None, None, :], axis=(1, 2))
    update = residual / (ab_energy[None, :] - pair_energy[:, None])
    return (residual, update)


def kernel(
    N, Z, T, W,
    amp, integ, cd_in, ab_in, allowed_in,
    res_out,
    cd, ab, allowed, small_sem, amp_sem,
    raw, wh, wl, gathered, ordered, near_lhs, side_lhs, far_lhs,
    own, from_edge, from_mid, from_in, fin, efin, base, ebuf, last, res,
    isem, ag_send, ag_recv, stream_send, edge_recv, mid_recv, back_send,
    fin_send, base_recv, efin_send, last_send, last_recv, out_sem,
):
    g = lax.axis_index("gx")
    z = lax.axis_index("row")
    rows, K = amp.shape
    half = rows // 2
    pk = rows // Z
    C = N // 2
    U = T // 2
    lower = z < Z // 2
    edge = jnp.logical_or(z == 0, z == Z - 1)
    inner = jnp.logical_not(edge)
    inward = jnp.where(lower, z + 1, z - 1)
    outward = jnp.where(lower, z - 1, z + 1)
    chip, core = g // 2, lax.rem(g, 2)

    def peer(c, i):
        there = lax.rem(chip // 2 + c // 2, 2) * 2 + lax.rem(lax.rem(chip, 2) + lax.rem(c, 2), 2)
        return there * 2 + (core if i == 0 else 1 - core)

    partner = peer(0, 1)

    def load(t):
        cols = pl.ds(pl.multiple_of(t * W, W), W)
        return pltpu.make_async_copy(integ.at[:, cols], raw.at[t], isem.at[t])

    def own_amp(h):
        return pltpu.make_async_copy(amp.at[pl.ds(h * half, half), :], gathered.at[g, h], amp_sem)

    own_amp(0).start()
    own_amp(1).start()
    small = [
        pltpu.make_async_copy(src, dst, small_sem.at[i])
        for i, (src, dst) in enumerate((
            (cd_in, cd), (ab_in, ab), (allowed_in, allowed)))
    ]
    for c in small:
        c.start()
    load(0).start()
    barrier = pltpu.get_barrier_semaphore()
    close = [partner, peer(1, 0), peer(2, 0)]
    for to in close:
        pl.semaphore_signal(barrier, inc=1, device_id={"gx": to}, device_id_type=MESH)
    pl.semaphore_signal(barrier, inc=1, device_id={"row": inward}, device_id_type=MESH)

    @pl.when(inner)
    def _():
        pl.semaphore_signal(barrier, inc=1, device_id={"row": outward}, device_id_type=MESH)

    def send_own(to, h):
        return pltpu.make_async_remote_copy(
            src_ref=gathered.at[g, h], dst_ref=gathered.at[g, h], send_sem=ag_send,
            recv_sem=ag_recv.at[h, g], device_id={"gx": to}, device_id_type=MESH)

    def relay(s, h):
        return pltpu.make_async_remote_copy(
            src_ref=gathered.at[s, h], dst_ref=gathered.at[s, h], send_sem=ag_send,
            recv_sem=ag_recv.at[h, s], device_id={"gx": partner}, device_id_type=MESH)

    def cross(s, h, to):
        return pltpu.make_async_remote_copy(
            src_ref=gathered.at[s, h], dst_ref=gathered.at[s, h], send_sem=ag_send,
            recv_sem=ag_recv.at[h, s], device_id={"gx": to}, device_id_type=MESH)

    across, along, opposite = peer(1, 0), peer(2, 0), peer(3, 0)

    def spread():
        for h in range(2):
            send_own(partner, h).start()
        for h in range(2):
            send_own(across, h).start()
            send_own(along, h).start()

    def forward_side():
        for h in range(2):
            relay(across, h).wait_recv()
            if h == 0:
                cross(across, h, along).start()
            relay(across, h).start()
            relay(along, h).wait_recv()
            if h == 1:
                cross(along, h, across).start()
            relay(along, h).start()

    def forward_diag():
        for h in range(2):
            relay(opposite, h).wait_recv()
            relay(opposite, h).start()

    def arrived(cs):
        for c in cs:
            for h in range(2):
                relay(peer(c, 1), h).wait_recv()

    def prepare(cs, lhs):
        n = len(cs)
        M = n * 2 * rows
        for k in range(Z):
            for j, c in enumerate(cs):
                for i in range(2):
                    at = ((k * n + j) * 2 + i) * pk
                    s = peer(c, i)
                    up, down = (Z - 1 - k) * pk, k * pk
                    x = jnp.where(
                        lower,
                        gathered[s, up // half, up % half:up % half + pk, :],
                        gathered[s, down // half, down % half:down % half + pk, :])
                    ordered[at:at + pk, :] = x
        x = ordered[0:M, :]
        hi = x.astype(jnp.bfloat16)
        lhs[0:M, :] = hi
        lhs[M:2 * M, :] = (x - hi.astype(jnp.float32)).astype(jnp.bfloat16)

    KB = K // BLK
    WB = W // BLK

    def split(t):
        for b in range(KB):
            for j in range(WB):
                m = allowed[cd[b], ab[t * WB + j]].astype(jnp.float32)
                x = raw[t, b * BLK:(b + 1) * BLK, j * BLK:(j + 1) * BLK] * m
                hi = x.astype(jnp.bfloat16)
                wh[t, b * BLK:(b + 1) * BLK, j * BLK:(j + 1) * BLK] = hi
                wl[t, b * BLK:(b + 1) * BLK, j * BLK:(j + 1) * BLK] = (x - hi.astype(jnp.float32)).astype(jnp.bfloat16)

    def send_piece(c, i, t):
        return pltpu.make_async_remote_copy(
            src_ref=efin.at[c * 2 + i, t], dst_ref=ebuf.at[g, t], send_sem=efin_send, recv_sem=last_recv.at[g],
            device_id={"gx": peer(c, i)}, device_id_type=MESH)

    def send_tile(k, c, t):
        return pltpu.make_async_remote_copy(
            src_ref=own.at[k, c, t], dst_ref=from_edge.at[k, c, t], send_sem=stream_send,
            recv_sem=edge_recv.at[k, c, t // 2], device_id={"row": inward}, device_id_type=MESH)

    def send_last(s):
        return pltpu.make_async_remote_copy(
            src_ref=ebuf.at[s], dst_ref=last.at[s], send_sem=last_send, recv_sem=last_recv.at[s],
            device_id={"row": inward}, device_id_type=MESH)

    def compute(cs, lhs, t, ready=()):
        n = len(cs)
        M = n * 2 * rows
        R = 2 * pk
        both = jnp.dot(lhs[...], wh[t], preferred_element_type=jnp.float32)
        tail = jnp.dot(lhs[0:M, :], wl[t], preferred_element_type=jnp.float32)
        total = both[0:M] + both[M:2 * M] + tail
        for k in range(Z):
            for j, c in enumerate(cs):
                own[k, c, t] = total[(k * n + j) * R:(k * n + j + 1) * R, :]

        for k, c in ready:
            send_tile(k, c, t).start()
        if ready:
            for j, c in enumerate(cs):
                for i in range(2):
                    at = ((2 * n + j) * 2 + i) * pk
                    if c == 0 and i == 0:
                        ebuf[g, t] = total[at:at + pk, :]
                    else:
                        efin[c * 2 + i, t] = total[at:at + pk, :]
                        send_piece(c, i, t).start()

    def unit(i):
        seg, u, b = i // (2 * U), lax.rem(i, 2 * U) // 2, lax.rem(i, 2)
        k = jnp.where(seg == 0, b, jnp.where(seg == 1, 0, jnp.where(seg == 2, b, 1)))
        c = jnp.where(seg == 0, 0, jnp.where(seg == 1, 1 + b, jnp.where(seg == 2, 3 - 2 * b, 2 + b)))
        return k, c, u

    def pair(u):
        return pl.ds(u * 2, 2)

    def edge_unit(k, c, u):
        return pltpu.make_async_remote_copy(
            src_ref=own.at[k, c, pair(u)], dst_ref=from_edge.at[k, c, pair(u)], send_sem=stream_send,
            recv_sem=edge_recv.at[k, c, u], device_id={"row": inward}, device_id_type=MESH)

    def mid_unit(k, c, u):
        return pltpu.make_async_remote_copy(
            src_ref=own.at[k, c, pair(u)], dst_ref=from_mid.at[k, c, pair(u)], send_sem=stream_send,
            recv_sem=mid_recv.at[k, c, u], device_id={"row": inward}, device_id_type=MESH)

    def back_unit(c, u):
        return pltpu.make_async_remote_copy(
            src_ref=own.at[Z - 1, c, pair(u)], dst_ref=from_in.at[c, pair(u)], send_sem=back_send,
            recv_sem=mid_recv.at[0, c, u], device_id={"row": outward}, device_id_type=MESH)

    def base_unit(c, i, u):
        return pltpu.make_async_remote_copy(
            src_ref=fin.at[c * 2 + i, pair(u)], dst_ref=base.at[g, pair(u)], send_sem=fin_send,
            recv_sem=base_recv.at[g], device_id={"gx": peer(c, i)}, device_id_type=MESH)

    def scatter(c, u, total):
        @pl.when(c == 0)
        def _():
            base[g, pair(u)] = total[:, 0:pk, :]

        @pl.when(c > 0)
        def _():
            fin[c * 2, pair(u)] = total[:, 0:pk, :]
            base_unit(c, 0, u).start()

        fin[c * 2 + 1, pair(u)] = total[:, pk:2 * pk, :]
        base_unit(c, 1, u).start()

    def take_edge(i):
        k, c, u = unit(i)
        edge_unit(k, c, u).wait_recv()
        own[k, c, pair(u)] = own[k, c, pair(u)] + from_edge[k, c, pair(u)]
        mid_unit(k, c, u).start()

    def take_mid(i):
        k, c, u = unit(i)
        mid_unit(k, c, u).wait_recv()

        @pl.when(k == 0)
        def _():
            own[Z - 1, c, pair(u)] = own[Z - 1, c, pair(u)] + from_mid[0, c, pair(u)]
            back_unit(c, u).start()

        @pl.when(k == 1)
        def _():
            scatter(c, u, own[Z - 2, c, pair(u)] + from_mid[1, c, pair(u)])

    def take_back(i):
        j = i - U
        c = jnp.where(i < U, 0, jnp.where(i < 3 * U, 1 + lax.rem(j + 2 * U, 2), 3))
        u = jnp.where(i < U, i, jnp.where(i < 3 * U, j // 2, i - 3 * U))
        back_unit(c, u).wait_recv()
        scatter(c, u, own[Z - 1, c, pair(u)] + from_in[c, pair(u)])

    def whole_ebuf(s):
        return pltpu.make_async_remote_copy(
            src_ref=ebuf.at[s], dst_ref=ebuf.at[s], send_sem=last_send, recv_sem=last_recv.at[s],
            device_id={"gx": s}, device_id_type=MESH)

    def whole_base(s):
        return pltpu.make_async_remote_copy(
            src_ref=base.at[s], dst_ref=base.at[s], send_sem=last_send, recv_sem=base_recv.at[s],
            device_id={"gx": s}, device_id_type=MESH)

    near, side, diag = (0,), (1, 2), (3,)
    n_units = 2 * C * U

    def repeat(lo, hi, body):
        def once(t, carry):
            body(t)
            return carry
        lax.fori_loop(lo, hi, once, 0)

    def ready_tile(t):
        load(t).wait()
        split(t)

    pltpu.make_async_copy(gathered.at[g], gathered.at[g], amp_sem).wait()
    for c in small:
        c.wait()
    repeat(1, T, lambda t: load(t).start())
    pl.semaphore_wait(barrier, len(close) + jnp.where(edge, 1, 2))
    spread()
    repeat(0, T // 2, ready_tile)
    for h in range(2):
        relay(partner, h).wait_recv()
    prepare(near, near_lhs)

    def tiles(ready):
        def late(t):
            ready_tile(t)
            compute(near, near_lhs, t, ready)

        repeat(0, T // 2, lambda t: compute(near, near_lhs, t, ready))
        repeat(T // 2, T - 2, late)
        forward_side()
        repeat(T - 2, T, late)
        arrived(side)
        prepare(side, side_lhs)

    @pl.when(edge)
    def _():
        tiles(((0, 0), (1, 0)))
        repeat(0, T - 2, lambda t: compute(side, side_lhs, t, ((0, 1), (0, 2))))
        forward_diag()
        repeat(T - 2, T, lambda t: compute(side, side_lhs, t, ((0, 1), (0, 2))))
        arrived(diag)
        prepare(diag, far_lhs)
        repeat(0, T, lambda t: compute(diag, far_lhs, t, ((0, 3), (1, 1))))

        def rest(u):
            for c in (2, 3):
                edge_unit(1, c, u).start()

        repeat(0, U, rest)
        send_last(g).start()
        for j in range(1, N):
            s_from = peer(j // 2, j % 2)
            whole_ebuf(s_from).wait_recv()
            send_last(s_from).start()
        repeat(0, n_units // 2, take_back)

    @pl.when(inner)
    def _():
        lag = jnp.where(lower, LAGS[0], LAGS[1])

        def middle(i):
            @pl.when(jnp.logical_and(i >= 0, i < n_units))
            def _():
                take_mid(i)

        def with_side(t):
            compute(side, side_lhs, t)
            take_edge(t)
            middle(t - lag)

        def with_diag(t):
            compute(diag, far_lhs, t)
            take_edge(T + t)
            middle(T + t - lag)

        def both(i):
            take_edge(i)
            middle(i - lag)

        tiles(())
        repeat(0, T - 2, with_side)
        forward_diag()
        repeat(T - 2, T, with_side)
        arrived(diag)
        prepare(diag, far_lhs)
        repeat(0, T, with_diag)
        repeat(2 * T, n_units, both)
        repeat(n_units, n_units + max(LAGS), lambda i: middle(i - lag))

    def put(s):
        band = pl.ds(pl.multiple_of(s * T * W, T * W), T * W)
        return pltpu.make_async_copy(res.at[:, band], res_out.at[:, band], out_sem)

    def finish(s):
        def place(t):
            return pl.ds(pl.multiple_of((s * T + t) * W, W), W)

        @pl.when(edge)
        def _():
            for t in range(T):
                res[:, place(t)] = base[s, t]

        @pl.when(inner)
        def _():
            send_last(s).wait_recv()
            for t in range(T):
                res[:, place(t)] = base[s, t] + last[s, t]

        put(s).start()

    finish(g)

    def collect(j, carry):
        c, i = j // 2, lax.rem(j, 2)
        s = lax.rem(chip // 2 + c // 2, 2) * 2 + lax.rem(lax.rem(chip, 2) + lax.rem(c, 2), 2)
        s = s * 2 + lax.rem(core + i, 2)
        whole_base(s).wait_recv()
        finish(s)
        return carry

    lax.fori_loop(1, N, collect, 0)

    pltpu.make_async_remote_copy(
        src_ref=gathered.at[0:N - 1], dst_ref=gathered.at[0:N - 1], send_sem=ag_send, recv_sem=ag_recv.at[0, 0],
        device_id={"gx": partner}, device_id_type=MESH).wait_send()

    pltpu.make_async_remote_copy(
        src_ref=own.at[0:2], dst_ref=from_edge, send_sem=stream_send, recv_sem=edge_recv.at[0, 0, 0],
        device_id={"row": inward}, device_id_type=MESH).wait_send()

    def sent(ref, sem):
        pltpu.make_async_remote_copy(
            src_ref=ref.at[1:N], dst_ref=ebuf.at[1:N], send_sem=sem, recv_sem=last_recv.at[0],
            device_id={"gx": partner}, device_id_type=MESH).wait_send()

    sent(fin, fin_send)

    @pl.when(edge)
    def _():
        sent(efin, efin_send)
        pltpu.make_async_remote_copy(
            src_ref=ebuf, dst_ref=last, send_sem=last_send, recv_sem=last_recv.at[g],
            device_id={"row": inward}, device_id_type=MESH).wait_send()

    @pl.when(inner)
    def _():
        pltpu.make_async_remote_copy(
            src_ref=own.at[Z - 1], dst_ref=from_in, send_sem=back_send, recv_sem=mid_recv.at[0, 0, 0],
            device_id={"row": outward}, device_id_type=MESH).wait_send()

    pltpu.make_async_copy(res, res_out, out_sem).wait()


def divide(res, pair_occ, occ, energy, res_out, upd_out):
    pk, A = res.shape
    which = lax.broadcasted_iota(jnp.int32, (pk, 1), 0)
    pe = jnp.zeros((pk, 1), jnp.float32)
    for k in range(pk):
        pe = jnp.where(which == k, occ[pair_occ[0, k]] + occ[pair_occ[1, k]], pe)
    v = res[...]
    res_out[...] = v
    upd_out[...] = v / (energy[...] - pe)


def fused_body(N, Z, W, amplitudes, integrals, cd_irrep, ab_irrep, allowed, pair_occ, occ_energy, ab_energy):
    rows, K = amplitudes.shape
    AB = integrals.shape[1]
    A = ab_energy.shape[0]
    T = AB // W
    U = T // 2
    C = N // 2
    pk = rows // Z
    R = 2 * pk
    vmem, smem = pltpu.VMEM, pltpu.SMEM
    f32, bf16, i32 = jnp.float32, jnp.bfloat16, jnp.int32
    dma = pltpu.SemaphoreType.DMA
    out = jax.ShapeDtypeStruct((pk, A), f32)
    residual = pl.pallas_call(
        functools.partial(kernel, N, Z, T, W),
        out_shape=out,
        in_specs=[pl.BlockSpec(memory_space=pltpu.HBM)] * 5,
        out_specs=pl.BlockSpec(memory_space=pltpu.HBM),
        scratch_shapes=[
            smem(cd_irrep.shape, i32), smem(ab_irrep.shape, i32), smem(allowed.shape, i32), dma((3,)), dma,
            vmem((T, K, W), f32), vmem((T, K, W), bf16), vmem((T, K, W), bf16),
            vmem((N, 2, rows // 2, K), f32), vmem((4 * rows, K), f32),
            vmem((4 * rows, K), bf16), vmem((8 * rows, K), bf16), vmem((4 * rows, K), bf16),
            vmem((Z, C, T, R, W), f32), vmem((2, C, T, R, W), f32), vmem((2, C, T, R, W), f32), vmem((C, T, R, W), f32),
            vmem((N, T, pk, W), f32), vmem((N, T, pk, W), f32),
            vmem((N, T, pk, W), f32), vmem((N, T, pk, W), f32), vmem((N, T, pk, W), f32), vmem((pk, A), f32),
            dma((T,)), dma, dma((2, N)), dma, dma((2, C, U)), dma((2, C, U)), dma,
            dma, dma((N,)), dma, dma, dma((N,)), dma,
        ],
        compiler_params=pltpu.CompilerParams(
            collective_id=0, has_side_effects=True, vmem_limit_bytes=VMEM_GRANT),
    )(amplitudes, integrals, cd_irrep, ab_irrep, allowed)
    return pl.pallas_call(
        divide,
        out_shape=(out, out),
        in_specs=[pl.BlockSpec(memory_space=s) for s in (vmem, smem, smem, vmem)],
        out_specs=[pl.BlockSpec(memory_space=vmem)] * 2,
        compiler_params=pltpu.CompilerParams(vmem_limit_bytes=VMEM_GRANT),
    )(residual, pair_occ.T, occ_energy, ab_energy.reshape(1, A))


def solution(mesh):
    N, Z = mesh.shape["gx"], mesh.shape["row"]

    def body(amplitudes, integrals, *rest):
        rows, K = amplitudes.shape
        AB = integrals.shape[1]
        W = 2 * BLK
        pk = rows // Z
        need = 8 * K * AB + 16 * rows * N * K + 16 * rows * N * AB + 28 * pk * AB * N
        if need > VMEM_BUDGET * 3 // 4 or AB % (2 * W) or N != 8 or Z != 4 or rows != 4 * Z:
            return plain_body(amplitudes, integrals, *rest)
        return fused_body(N, Z, W, amplitudes, integrals, *rest)

    return jax.shard_map(
        body,
        mesh=mesh,
        in_specs=(
            P("gx", "row"),
            P("row", "gx"),
            P("row"),
            P("gx"),
            P(),
            P(("gx", "row"), None),
            P(),
            P(),
        ),
        out_specs=(P(("gx", "row"), None), P(("gx", "row"), None)),
        check_vma=False,
    )
```

```python
import functools

import jax
import jax.numpy as jnp
from jax import lax
from jax.experimental import pallas as pl
from jax.experimental.pallas import tpu as pltpu
from jax.sharding import PartitionSpec as P

BLK = 128
MESH = pl.DeviceIdType.MESH
VMEM_BUDGET = 48 * 2**20
VMEM_GRANT = 67043328
LAGS = (11, 5)


def plain_body(amplitudes, integrals, cd_irrep, ab_irrep, allowed, pair_occ, occ_energy, ab_energy):
    irrep_labels = jnp.arange(allowed.shape[0], dtype=jnp.int32)
    cd_onehot = (cd_irrep[:, None] == irrep_labels[None, :]).astype(jnp.float32)
    ab_onehot = (ab_irrep[:, None] == irrep_labels[None, :]).astype(jnp.float32)
    irrep_table = allowed.astype(jnp.float32)
    block_mask = jnp.dot(
        jnp.dot(cd_onehot, irrep_table, precision=lax.Precision.HIGHEST),
        ab_onehot.T,
        precision=lax.Precision.HIGHEST,
    )
    cd_rows, ab_cols = integrals.shape
    effective = (
        integrals.reshape(cd_rows // BLK, BLK, ab_cols // BLK, BLK) * block_mask[:, None, :, None]
    ).reshape(cd_rows, ab_cols)
    partial_value = jnp.dot(
        lax.all_gather(amplitudes, "gx", axis=0, tiled=True),
        effective,
        precision=lax.Precision.HIGHEST,
        preferred_element_type=jnp.float32,
    )
    arrived = lax.all_to_all(partial_value, "gx", split_axis=0, concat_axis=1, tiled=True)
    residual = lax.psum_scatter(arrived, "row", scatter_dimension=0, tiled=True)
    occ_labels = jnp.arange(occ_energy.shape[0], dtype=jnp.int32)
    pair_onehot = (pair_occ[:, :, None] == occ_labels[None, None, :]).astype(jnp.float32)
    pair_energy = jnp.sum(pair_onehot * occ_energy[None, None, :], axis=(1, 2))
    update = residual / (ab_energy[None, :] - pair_energy[:, None])
    return (residual, update)


def kernel(
    N, Z, T, W,
    amp, integ, cd_in, ab_in, allowed_in,
    res_out,
    cd, ab, allowed, small_sem, amp_sem,
    raw, wh, wl, gathered, ordered, near_lhs, side_lhs, far_lhs,
    own, from_edge, from_mid, from_in, fin, efin, base, ebuf, last, res,
    isem, ag_send, ag_recv, stream_send, edge_recv, mid_recv, back_send,
    fin_send, base_recv, efin_send, last_send, last_recv, out_sem,
):
    g = lax.axis_index("gx")
    z = lax.axis_index("row")
    rows, K = amp.shape
    half = rows // 2
    pk = rows // Z
    C = N // 2
    U = T // 2
    lower = z < Z // 2
    edge = jnp.logical_or(z == 0, z == Z - 1)
    inner = jnp.logical_not(edge)
    inward = jnp.where(lower, z + 1, z - 1)
    outward = jnp.where(lower, z - 1, z + 1)
    chip, core = g // 2, lax.rem(g, 2)

    def peer(c, i):
        there = lax.rem(chip // 2 + c // 2, 2) * 2 + lax.rem(lax.rem(chip, 2) + lax.rem(c, 2), 2)
        return there * 2 + (core if i == 0 else 1 - core)

    partner = peer(0, 1)

    def load(t):
        cols = pl.ds(pl.multiple_of(t * W, W), W)
        return pltpu.make_async_copy(integ.at[:, cols], raw.at[t], isem.at[t])

    def own_amp(h):
        return pltpu.make_async_copy(amp.at[pl.ds(h * half, half), :], gathered.at[g, h], amp_sem)

    own_amp(0).start()
    own_amp(1).start()
    small = [
        pltpu.make_async_copy(src, dst, small_sem.at[i])
        for i, (src, dst) in enumerate((
            (cd_in, cd), (ab_in, ab), (allowed_in, allowed)))
    ]
    for c in small:
        c.start()
    first, split_first = 1, 2
    for t in range(first):
        load(t).start()
    barrier = pltpu.get_barrier_semaphore()
    close = [partner, peer(1, 0), peer(2, 0)]
    for to in close:
        pl.semaphore_signal(barrier, inc=1, device_id={"gx": to}, device_id_type=MESH)
    pl.semaphore_signal(barrier, inc=1, device_id={"row": inward}, device_id_type=MESH)

    @pl.when(inner)
    def _():
        pl.semaphore_signal(barrier, inc=1, device_id={"row": outward}, device_id_type=MESH)

    def send_own(to, h):
        return pltpu.make_async_remote_copy(
            src_ref=gathered.at[g, h], dst_ref=gathered.at[g, h], send_sem=ag_send,
            recv_sem=ag_recv.at[h, g], device_id={"gx": to}, device_id_type=MESH)

    def relay(s, h):
        return pltpu.make_async_remote_copy(
            src_ref=gathered.at[s, h], dst_ref=gathered.at[s, h], send_sem=ag_send,
            recv_sem=ag_recv.at[h, s], device_id={"gx": partner}, device_id_type=MESH)

    def cross(s, h, to):
        return pltpu.make_async_remote_copy(
            src_ref=gathered.at[s, h], dst_ref=gathered.at[s, h], send_sem=ag_send,
            recv_sem=ag_recv.at[h, s], device_id={"gx": to}, device_id_type=MESH)

    across, along, opposite = peer(1, 0), peer(2, 0), peer(3, 0)

    def spread():
        for h in range(2):
            send_own(partner, h).start()
        for to, h in ((across, 0), (along, 1), (across, 1), (along, 0)):
            send_own(to, h).start()

    def forward_cross():
        relay(across, 0).wait_recv()
        cross(across, 0, along).start()
        relay(across, 0).start()
        relay(along, 1).wait_recv()
        cross(along, 1, across).start()
        relay(along, 1).start()

    def forward_side():
        relay(across, 1).wait_recv()
        relay(across, 1).start()
        relay(along, 0).wait_recv()
        relay(along, 0).start()

    def forward_diag():
        for h in range(2):
            relay(opposite, h).wait_recv()
            relay(opposite, h).start()

    def arrived(cs):
        for c in cs:
            for h in range(2):
                relay(peer(c, 1), h).wait_recv()

    def prepare(cs, lhs):
        n = len(cs)
        M = n * 2 * rows
        for k in range(Z):
            for j, c in enumerate(cs):
                for i in range(2):
                    at = ((k * n + j) * 2 + i) * pk
                    s = peer(c, i)
                    up, down = (Z - 1 - k) * pk, k * pk
                    x = jnp.where(
                        lower,
                        gathered[s, up // half, up % half:up % half + pk, :],
                        gathered[s, down // half, down % half:down % half + pk, :])
                    ordered[at:at + pk, :] = x
        x = ordered[0:M, :]
        hi = x.astype(jnp.bfloat16)
        lhs[0:M, :] = hi
        lhs[M:2 * M, :] = (x - hi.astype(jnp.float32)).astype(jnp.bfloat16)

    KB = K // BLK
    WB = W // BLK

    def split(t):
        for b in range(KB):
            for j in range(WB):
                m = allowed[cd[b], ab[t * WB + j]].astype(jnp.float32)
                x = raw[t, b * BLK:(b + 1) * BLK, j * BLK:(j + 1) * BLK] * m
                hi = x.astype(jnp.bfloat16)
                wh[t, b * BLK:(b + 1) * BLK, j * BLK:(j + 1) * BLK] = hi
                wl[t, b * BLK:(b + 1) * BLK, j * BLK:(j + 1) * BLK] = (x - hi.astype(jnp.float32)).astype(jnp.bfloat16)

    def send_piece(c, i, t):
        return pltpu.make_async_remote_copy(
            src_ref=efin.at[c * 2 + i, t], dst_ref=ebuf.at[g, t], send_sem=efin_send, recv_sem=last_recv.at[g],
            device_id={"gx": peer(c, i)}, device_id_type=MESH)

    def send_tile(k, c, t):
        return pltpu.make_async_remote_copy(
            src_ref=own.at[k, c, t], dst_ref=from_edge.at[k, c, t], send_sem=stream_send,
            recv_sem=edge_recv.at[k, c, t // 2], device_id={"row": inward}, device_id_type=MESH)

    def send_last(s):
        return pltpu.make_async_remote_copy(
            src_ref=ebuf.at[s], dst_ref=last.at[s], send_sem=last_send, recv_sem=last_recv.at[s],
            device_id={"row": inward}, device_id_type=MESH)

    def compute(cs, lhs, t, ready=()):
        n = len(cs)
        M = n * 2 * rows
        R = 2 * pk
        both = jnp.dot(lhs[...], wh[t], preferred_element_type=jnp.float32)
        tail = jnp.dot(lhs[0:M, :], wl[t], preferred_element_type=jnp.float32)
        total = both[0:M] + both[M:2 * M] + tail
        for k in range(Z):
            for j, c in enumerate(cs):
                own[k, c, t] = total[(k * n + j) * R:(k * n + j + 1) * R, :]

        for k, c in ready:
            send_tile(k, c, t).start()
        if ready:
            for j, c in enumerate(cs):
                for i in range(2):
                    at = ((2 * n + j) * 2 + i) * pk
                    if c == 0 and i == 0:
                        ebuf[g, t] = total[at:at + pk, :]
                    else:
                        efin[c * 2 + i, t] = total[at:at + pk, :]
                        send_piece(c, i, t).start()

    def unit(i):
        seg, u, b = i // (2 * U), lax.rem(i, 2 * U) // 2, lax.rem(i, 2)
        k = jnp.where(seg == 0, b, jnp.where(seg == 1, 0, jnp.where(seg == 2, b, 1)))
        c = jnp.where(seg == 0, 0, jnp.where(seg == 1, 1 + b, jnp.where(seg == 2, 3 - 2 * b, 2 + b)))
        return k, c, u

    def pair(u):
        return pl.ds(u * 2, 2)

    def edge_unit(k, c, u):
        return pltpu.make_async_remote_copy(
            src_ref=own.at[k, c, pair(u)], dst_ref=from_edge.at[k, c, pair(u)], send_sem=stream_send,
            recv_sem=edge_recv.at[k, c, u], device_id={"row": inward}, device_id_type=MESH)

    def mid_unit(k, c, u):
        return pltpu.make_async_remote_copy(
            src_ref=own.at[k, c, pair(u)], dst_ref=from_mid.at[k, c, pair(u)], send_sem=stream_send,
            recv_sem=mid_recv.at[k, c, u], device_id={"row": inward}, device_id_type=MESH)

    def back_unit(c, u):
        return pltpu.make_async_remote_copy(
            src_ref=own.at[Z - 1, c, pair(u)], dst_ref=from_in.at[c, pair(u)], send_sem=back_send,
            recv_sem=mid_recv.at[0, c, u], device_id={"row": outward}, device_id_type=MESH)

    def base_unit(c, i, u):
        return pltpu.make_async_remote_copy(
            src_ref=fin.at[c * 2 + i, pair(u)], dst_ref=base.at[g, pair(u)], send_sem=fin_send,
            recv_sem=base_recv.at[g], device_id={"gx": peer(c, i)}, device_id_type=MESH)

    def scatter(c, u, total):
        @pl.when(c == 0)
        def _():
            base[g, pair(u)] = total[:, 0:pk, :]

        @pl.when(c > 0)
        def _():
            fin[c * 2, pair(u)] = total[:, 0:pk, :]
            base_unit(c, 0, u).start()

        fin[c * 2 + 1, pair(u)] = total[:, pk:2 * pk, :]
        base_unit(c, 1, u).start()

    def take_edge(i):
        k, c, u = unit(i)
        edge_unit(k, c, u).wait_recv()
        own[k, c, pair(u)] = own[k, c, pair(u)] + from_edge[k, c, pair(u)]
        mid_unit(k, c, u).start()

    def take_mid(i):
        k, c, u = unit(i)
        mid_unit(k, c, u).wait_recv()

        @pl.when(k == 0)
        def _():
            own[Z - 1, c, pair(u)] = own[Z - 1, c, pair(u)] + from_mid[0, c, pair(u)]
            back_unit(c, u).start()

        @pl.when(k == 1)
        def _():
            scatter(c, u, own[Z - 2, c, pair(u)] + from_mid[1, c, pair(u)])

    def take_back(i):
        j = i - U
        c = jnp.where(i < U, 0, jnp.where(i < 3 * U, 1 + lax.rem(j + 2 * U, 2), 3))
        u = jnp.where(i < U, i, jnp.where(i < 3 * U, j // 2, i - 3 * U))
        back_unit(c, u).wait_recv()
        scatter(c, u, own[Z - 1, c, pair(u)] + from_in[c, pair(u)])

    def whole_ebuf(s):
        return pltpu.make_async_remote_copy(
            src_ref=ebuf.at[s], dst_ref=ebuf.at[s], send_sem=last_send, recv_sem=last_recv.at[s],
            device_id={"gx": s}, device_id_type=MESH)

    def whole_base(s):
        return pltpu.make_async_remote_copy(
            src_ref=base.at[s], dst_ref=base.at[s], send_sem=last_send, recv_sem=base_recv.at[s],
            device_id={"gx": s}, device_id_type=MESH)

    near, side, diag = (0,), (1, 2), (3,)
    n_units = 2 * C * U

    def repeat(lo, hi, body):
        def once(t, carry):
            body(t)
            return carry
        lax.fori_loop(lo, hi, once, 0)

    def ready_tile(t):
        load(t).wait()
        split(t)

    pltpu.make_async_copy(gathered.at[g], gathered.at[g], amp_sem).wait()
    for c in small:
        c.wait()
    repeat(first, T, lambda t: load(t).start())
    pl.semaphore_wait(barrier, len(close) + jnp.where(edge, 1, 2))
    spread()
    repeat(0, split_first, ready_tile)
    for h in range(2):
        relay(partner, h).wait_recv()
    prepare(near, near_lhs)

    def tiles(ready):
        def late(t):
            ready_tile(t)
            compute(near, near_lhs, t, ready)

        repeat(0, split_first, lambda t: compute(near, near_lhs, t, ready))
        repeat(split_first, T // 2 + 1, late)
        forward_cross()
        repeat(T // 2 + 1, T - 2, late)
        forward_side()
        repeat(T - 2, T, late)
        arrived(side)
        prepare(side, side_lhs)

    @pl.when(edge)
    def _():
        tiles(((0, 0), (1, 0)))
        repeat(0, T - 3, lambda t: compute(side, side_lhs, t, ((0, 1), (0, 2))))
        forward_diag()
        repeat(T - 3, T, lambda t: compute(side, side_lhs, t, ((0, 1), (0, 2))))
        arrived(diag)
        prepare(diag, far_lhs)
        repeat(0, T, lambda t: compute(diag, far_lhs, t, ((0, 3), (1, 1))))

        def rest(u):
            for c in (2, 3):
                edge_unit(1, c, u).start()

        repeat(0, U, rest)
        send_last(g).start()
        for j in range(1, N):
            s_from = peer(j // 2, j % 2)
            whole_ebuf(s_from).wait_recv()
            send_last(s_from).start()
        repeat(0, n_units // 2, take_back)

    @pl.when(inner)
    def _():
        lag = jnp.where(lower, LAGS[0], LAGS[1])

        def middle(i):
            @pl.when(jnp.logical_and(i >= 0, i < n_units))
            def _():
                take_mid(i)

        def with_side(t):
            compute(side, side_lhs, t)
            take_edge(t)
            middle(t - lag)

        def with_diag(t):
            compute(diag, far_lhs, t)
            take_edge(T + t)
            middle(T + t - lag)

        def both(i):
            take_edge(i)
            middle(i - lag)

        tiles(())
        repeat(0, T - 3, with_side)
        forward_diag()
        repeat(T - 3, T, with_side)
        arrived(diag)
        prepare(diag, far_lhs)
        repeat(0, T, with_diag)
        repeat(2 * T, n_units, both)
        repeat(n_units, n_units + max(LAGS), lambda i: middle(i - lag))

    def put(s):
        band = pl.ds(pl.multiple_of(s * T * W, T * W), T * W)
        return pltpu.make_async_copy(res.at[:, band], res_out.at[:, band], out_sem)

    def finish(s):
        def place(t):
            return pl.ds(pl.multiple_of((s * T + t) * W, W), W)

        @pl.when(edge)
        def _():
            for t in range(T):
                res[:, place(t)] = base[s, t]

        @pl.when(inner)
        def _():
            send_last(s).wait_recv()
            for t in range(T):
                res[:, place(t)] = base[s, t] + last[s, t]

        put(s).start()

    finish(g)

    def collect(j, carry):
        c, i = j // 2, lax.rem(j, 2)
        s = lax.rem(chip // 2 + c // 2, 2) * 2 + lax.rem(lax.rem(chip, 2) + lax.rem(c, 2), 2)
        s = s * 2 + lax.rem(core + i, 2)
        whole_base(s).wait_recv()
        finish(s)
        return carry

    lax.fori_loop(1, N, collect, 0)

    pltpu.make_async_remote_copy(
        src_ref=gathered.at[0:N - 1], dst_ref=gathered.at[0:N - 1], send_sem=ag_send, recv_sem=ag_recv.at[0, 0],
        device_id={"gx": partner}, device_id_type=MESH).wait_send()

    pltpu.make_async_remote_copy(
        src_ref=own.at[0:2], dst_ref=from_edge, send_sem=stream_send, recv_sem=edge_recv.at[0, 0, 0],
        device_id={"row": inward}, device_id_type=MESH).wait_send()

    def sent(ref, sem):
        pltpu.make_async_remote_copy(
            src_ref=ref.at[1:N], dst_ref=ebuf.at[1:N], send_sem=sem, recv_sem=last_recv.at[0],
            device_id={"gx": partner}, device_id_type=MESH).wait_send()

    sent(fin, fin_send)

    @pl.when(edge)
    def _():
        sent(efin, efin_send)
        pltpu.make_async_remote_copy(
            src_ref=ebuf, dst_ref=last, send_sem=last_send, recv_sem=last_recv.at[g],
            device_id={"row": inward}, device_id_type=MESH).wait_send()

    @pl.when(inner)
    def _():
        pltpu.make_async_remote_copy(
            src_ref=own.at[Z - 1], dst_ref=from_in, send_sem=back_send, recv_sem=mid_recv.at[0, 0, 0],
            device_id={"row": outward}, device_id_type=MESH).wait_send()

    pltpu.make_async_copy(res, res_out, out_sem).wait()


def divide(res, pair_occ, occ, energy, res_out, upd_out):
    pk, A = res.shape
    which = lax.broadcasted_iota(jnp.int32, (pk, 1), 0)
    pe = jnp.zeros((pk, 1), jnp.float32)
    for k in range(pk):
        pe = jnp.where(which == k, occ[pair_occ[0, k]] + occ[pair_occ[1, k]], pe)
    v = res[...]
    res_out[...] = v
    upd_out[...] = v / (energy[...] - pe)


def fused_body(N, Z, W, amplitudes, integrals, cd_irrep, ab_irrep, allowed, pair_occ, occ_energy, ab_energy):
    rows, K = amplitudes.shape
    AB = integrals.shape[1]
    A = ab_energy.shape[0]
    T = AB // W
    U = T // 2
    C = N // 2
    pk = rows // Z
    R = 2 * pk
    vmem, smem = pltpu.VMEM, pltpu.SMEM
    f32, bf16, i32 = jnp.float32, jnp.bfloat16, jnp.int32
    dma = pltpu.SemaphoreType.DMA
    out = jax.ShapeDtypeStruct((pk, A), f32)
    residual = pl.pallas_call(
        functools.partial(kernel, N, Z, T, W),
        out_shape=out,
        in_specs=[pl.BlockSpec(memory_space=pltpu.HBM)] * 5,
        out_specs=pl.BlockSpec(memory_space=pltpu.HBM),
        scratch_shapes=[
            smem(cd_irrep.shape, i32), smem(ab_irrep.shape, i32), smem(allowed.shape, i32), dma((3,)), dma,
            vmem((T, K, W), f32), vmem((T, K, W), bf16), vmem((T, K, W), bf16),
            vmem((N, 2, rows // 2, K), f32), vmem((4 * rows, K), f32),
            vmem((4 * rows, K), bf16), vmem((8 * rows, K), bf16), vmem((4 * rows, K), bf16),
            vmem((Z, C, T, R, W), f32), vmem((2, C, T, R, W), f32), vmem((2, C, T, R, W), f32), vmem((C, T, R, W), f32),
            vmem((N, T, pk, W), f32), vmem((N, T, pk, W), f32),
            vmem((N, T, pk, W), f32), vmem((N, T, pk, W), f32), vmem((N, T, pk, W), f32), vmem((pk, A), f32),
            dma((T,)), dma, dma((2, N)), dma, dma((2, C, U)), dma((2, C, U)), dma,
            dma, dma((N,)), dma, dma, dma((N,)), dma,
        ],
        compiler_params=pltpu.CompilerParams(
            collective_id=0, has_side_effects=True, vmem_limit_bytes=VMEM_GRANT),
    )(amplitudes, integrals, cd_irrep, ab_irrep, allowed)
    return pl.pallas_call(
        divide,
        out_shape=(out, out),
        in_specs=[pl.BlockSpec(memory_space=s) for s in (vmem, smem, smem, vmem)],
        out_specs=[pl.BlockSpec(memory_space=vmem)] * 2,
        compiler_params=pltpu.CompilerParams(vmem_limit_bytes=VMEM_GRANT),
    )(residual, pair_occ.T, occ_energy, ab_energy.reshape(1, A))


def solution(mesh):
    N, Z = mesh.shape["gx"], mesh.shape["row"]

    def body(amplitudes, integrals, *rest):
        rows, K = amplitudes.shape
        AB = integrals.shape[1]
        W = 2 * BLK
        pk = rows // Z
        need = 8 * K * AB + 16 * rows * N * K + 16 * rows * N * AB + 28 * pk * AB * N
        if need > VMEM_BUDGET * 3 // 4 or AB % (2 * W) or AB < 6 * W or N != 8 or Z != 4 or rows != 4 * Z:
            return plain_body(amplitudes, integrals, *rest)
        return fused_body(N, Z, W, amplitudes, integrals, *rest)

    return jax.shard_map(
        body,
        mesh=mesh,
        in_specs=(
            P("gx", "row"),
            P("row", "gx"),
            P("row"),
            P("gx"),
            P(),
            P(("gx", "row"), None),
            P(),
            P(),
        ),
        out_specs=(P(("gx", "row"), None), P(("gx", "row"), None)),
        check_vma=False,
    )
```

```python
import functools

import jax
import jax.numpy as jnp
from jax import lax
from jax.experimental import pallas as pl
from jax.experimental.pallas import tpu as pltpu
from jax.sharding import PartitionSpec as P

BLK = 128
MESH = pl.DeviceIdType.MESH
VMEM_BUDGET = 48 * 2**20
VMEM_GRANT = 67043328
LAGS = (11, 5)


def plain_body(amplitudes, integrals, cd_irrep, ab_irrep, allowed, pair_occ, occ_energy, ab_energy):
    irrep_labels = jnp.arange(allowed.shape[0], dtype=jnp.int32)
    cd_onehot = (cd_irrep[:, None] == irrep_labels[None, :]).astype(jnp.float32)
    ab_onehot = (ab_irrep[:, None] == irrep_labels[None, :]).astype(jnp.float32)
    irrep_table = allowed.astype(jnp.float32)
    block_mask = jnp.dot(
        jnp.dot(cd_onehot, irrep_table, precision=lax.Precision.HIGHEST),
        ab_onehot.T,
        precision=lax.Precision.HIGHEST,
    )
    cd_rows, ab_cols = integrals.shape
    effective = (
        integrals.reshape(cd_rows // BLK, BLK, ab_cols // BLK, BLK) * block_mask[:, None, :, None]
    ).reshape(cd_rows, ab_cols)
    partial_value = jnp.dot(
        lax.all_gather(amplitudes, "gx", axis=0, tiled=True),
        effective,
        precision=lax.Precision.HIGHEST,
        preferred_element_type=jnp.float32,
    )
    arrived = lax.all_to_all(partial_value, "gx", split_axis=0, concat_axis=1, tiled=True)
    residual = lax.psum_scatter(arrived, "row", scatter_dimension=0, tiled=True)
    occ_labels = jnp.arange(occ_energy.shape[0], dtype=jnp.int32)
    pair_onehot = (pair_occ[:, :, None] == occ_labels[None, None, :]).astype(jnp.float32)
    pair_energy = jnp.sum(pair_onehot * occ_energy[None, None, :], axis=(1, 2))
    update = residual / (ab_energy[None, :] - pair_energy[:, None])
    return (residual, update)


def kernel(
    N, Z, T, W,
    amp, integ, cd_in, ab_in, allowed_in,
    res_out,
    cd, ab, allowed, small_sem, amp_sem,
    raw, wh, wl, gathered, ordered, near_lhs, side_lhs, far_lhs,
    own, from_edge, from_mid, from_in, fin, efin, base, ebuf, last, res,
    isem, ag_send, ag_recv, stream_send, edge_recv, mid_recv, back_send,
    fin_send, base_recv, efin_send, last_send, last_recv, out_sem,
):
    g = lax.axis_index("gx")
    z = lax.axis_index("row")
    rows, K = amp.shape
    half = rows // 2
    pk = rows // Z
    C = N // 2
    U = T // 2
    lower = z < Z // 2
    edge = jnp.logical_or(z == 0, z == Z - 1)
    inner = jnp.logical_not(edge)
    inward = jnp.where(lower, z + 1, z - 1)
    outward = jnp.where(lower, z - 1, z + 1)
    chip, core = g // 2, lax.rem(g, 2)

    def peer(c, i):
        there = lax.rem(chip // 2 + c // 2, 2) * 2 + lax.rem(lax.rem(chip, 2) + lax.rem(c, 2), 2)
        return there * 2 + (core if i == 0 else 1 - core)

    partner = peer(0, 1)

    def load(t):
        cols = pl.ds(pl.multiple_of(t * W, W), W)
        return pltpu.make_async_copy(integ.at[:, cols], raw.at[t], isem.at[t])

    def own_amp(h):
        return pltpu.make_async_copy(amp.at[pl.ds(h * half, half), :], gathered.at[g, h], amp_sem)

    own_amp(0).start()
    own_amp(1).start()
    small = [
        pltpu.make_async_copy(src, dst, small_sem.at[i])
        for i, (src, dst) in enumerate((
            (cd_in, cd), (ab_in, ab), (allowed_in, allowed)))
    ]
    for c in small:
        c.start()
    first, split_first = 1, 2
    for t in range(first):
        load(t).start()
    barrier = pltpu.get_barrier_semaphore()
    close = [partner, peer(1, 0), peer(2, 0)]
    for to in close:
        pl.semaphore_signal(barrier, inc=1, device_id={"gx": to}, device_id_type=MESH)
    pl.semaphore_signal(barrier, inc=1, device_id={"row": inward}, device_id_type=MESH)

    @pl.when(inner)
    def _():
        pl.semaphore_signal(barrier, inc=1, device_id={"row": outward}, device_id_type=MESH)

    def send_own(to, h):
        return pltpu.make_async_remote_copy(
            src_ref=gathered.at[g, h], dst_ref=gathered.at[g, h], send_sem=ag_send,
            recv_sem=ag_recv.at[h, g], device_id={"gx": to}, device_id_type=MESH)

    def relay(s, h):
        return pltpu.make_async_remote_copy(
            src_ref=gathered.at[s, h], dst_ref=gathered.at[s, h], send_sem=ag_send,
            recv_sem=ag_recv.at[h, s], device_id={"gx": partner}, device_id_type=MESH)

    def cross(s, h, to):
        return pltpu.make_async_remote_copy(
            src_ref=gathered.at[s, h], dst_ref=gathered.at[s, h], send_sem=ag_send,
            recv_sem=ag_recv.at[h, s], device_id={"gx": to}, device_id_type=MESH)

    across, along, opposite = peer(1, 0), peer(2, 0), peer(3, 0)

    def spread():
        for h in range(2):
            send_own(partner, h).start()
        for to, h in ((across, 0), (along, 1), (across, 1), (along, 0)):
            send_own(to, h).start()

    def forward_cross():
        relay(across, 0).wait_recv()
        cross(across, 0, along).start()
        relay(across, 0).start()
        relay(along, 1).wait_recv()
        cross(along, 1, across).start()
        relay(along, 1).start()

    def forward_side():
        relay(across, 1).wait_recv()
        relay(across, 1).start()
        relay(along, 0).wait_recv()
        relay(along, 0).start()

    def forward_diag():
        for h in range(2):
            relay(opposite, h).wait_recv()
            relay(opposite, h).start()

    def arrived(cs):
        for c in cs:
            for h in range(2):
                relay(peer(c, 1), h).wait_recv()

    def prepare(cs, lhs):
        n = len(cs)
        M = n * 2 * rows
        for k in range(Z):
            for j, c in enumerate(cs):
                for i in range(2):
                    at = ((k * n + j) * 2 + i) * pk
                    s = peer(c, i)
                    up, down = (Z - 1 - k) * pk, k * pk
                    x = jnp.where(
                        lower,
                        gathered[s, up // half, up % half:up % half + pk, :],
                        gathered[s, down // half, down % half:down % half + pk, :])
                    ordered[at:at + pk, :] = x
        x = ordered[0:M, :]
        hi = x.astype(jnp.bfloat16)
        lhs[0:M, :] = hi
        lhs[M:2 * M, :] = (x - hi.astype(jnp.float32)).astype(jnp.bfloat16)

    KB = K // BLK
    WB = W // BLK

    def split(t):
        for b in range(KB):
            for j in range(WB):
                m = allowed[cd[b], ab[t * WB + j]].astype(jnp.float32)
                x = raw[t, b * BLK:(b + 1) * BLK, j * BLK:(j + 1) * BLK] * m
                hi = x.astype(jnp.bfloat16)
                wh[t, b * BLK:(b + 1) * BLK, j * BLK:(j + 1) * BLK] = hi
                wl[t, b * BLK:(b + 1) * BLK, j * BLK:(j + 1) * BLK] = (x - hi.astype(jnp.float32)).astype(jnp.bfloat16)

    def send_piece(c, i, u):
        return pltpu.make_async_remote_copy(
            src_ref=efin.at[c * 2 + i, pair(u)], dst_ref=ebuf.at[g, pair(u)], send_sem=efin_send,
            recv_sem=last_recv.at[g], device_id={"gx": peer(c, i)}, device_id_type=MESH)

    def exchange(u):
        for c in range(C):
            both = own[2, c, pair(u)]
            for i in range(2):
                if c or i:
                    efin[c * 2 + i, pair(u)] = both[:, i * pk:(i + 1) * pk, :]
                    send_piece(c, i, u).start()

    def send_tile(k, c, t):
        return pltpu.make_async_remote_copy(
            src_ref=own.at[k, c, t], dst_ref=from_edge.at[k, c, t], send_sem=stream_send,
            recv_sem=edge_recv.at[k, c, t // 2], device_id={"row": inward}, device_id_type=MESH)

    def send_last(s):
        return pltpu.make_async_remote_copy(
            src_ref=ebuf.at[s], dst_ref=last.at[s], send_sem=last_send, recv_sem=last_recv.at[s],
            device_id={"row": inward}, device_id_type=MESH)

    def compute(cs, lhs, t, ready=()):
        n = len(cs)
        M = n * 2 * rows
        R = 2 * pk
        both = jnp.dot(lhs[...], wh[t], preferred_element_type=jnp.float32)
        tail = jnp.dot(lhs[0:M, :], wl[t], preferred_element_type=jnp.float32)
        total = both[0:M] + both[M:2 * M] + tail
        for k in range(Z):
            for j, c in enumerate(cs):
                own[k, c, t] = total[(k * n + j) * R:(k * n + j + 1) * R, :]

        for k, c in ready:
            send_tile(k, c, t).start()
        if ready and cs[0] == 0:
            at = 4 * n * pk
            ebuf[g, t] = total[at:at + pk, :]

    def unit(i):
        seg, r = i // (2 * U), lax.rem(i, 2 * U)
        u = jnp.where(seg == 2, lax.rem(r, U), r // 2)
        b = jnp.where(seg == 2, r // U, lax.rem(r, 2))
        k = jnp.where(seg == 0, b, jnp.where(seg == 1, 0, jnp.where(seg == 2, b, 1)))
        c = jnp.where(seg == 0, 0, jnp.where(seg == 1, 1 + b, jnp.where(seg == 2, 3 - 2 * b, 2 + b)))
        return k, c, u

    def pair(u):
        return pl.ds(u * 2, 2)

    def edge_unit(k, c, u):
        return pltpu.make_async_remote_copy(
            src_ref=own.at[k, c, pair(u)], dst_ref=from_edge.at[k, c, pair(u)], send_sem=stream_send,
            recv_sem=edge_recv.at[k, c, u], device_id={"row": inward}, device_id_type=MESH)

    def mid_unit(k, c, u):
        return pltpu.make_async_remote_copy(
            src_ref=own.at[k, c, pair(u)], dst_ref=from_mid.at[k, c, pair(u)], send_sem=stream_send,
            recv_sem=mid_recv.at[k, c, u], device_id={"row": inward}, device_id_type=MESH)

    def back_unit(c, u):
        return pltpu.make_async_remote_copy(
            src_ref=own.at[Z - 1, c, pair(u)], dst_ref=from_in.at[c, pair(u)], send_sem=back_send,
            recv_sem=mid_recv.at[0, c, u], device_id={"row": outward}, device_id_type=MESH)

    def base_unit(c, i, u):
        return pltpu.make_async_remote_copy(
            src_ref=fin.at[c * 2 + i, pair(u)], dst_ref=base.at[g, pair(u)], send_sem=fin_send,
            recv_sem=base_recv.at[g], device_id={"gx": peer(c, i)}, device_id_type=MESH)

    def scatter(c, u, total):
        @pl.when(c == 0)
        def _():
            base[g, pair(u)] = total[:, 0:pk, :]

        @pl.when(c > 0)
        def _():
            fin[c * 2, pair(u)] = total[:, 0:pk, :]
            base_unit(c, 0, u).start()

        fin[c * 2 + 1, pair(u)] = total[:, pk:2 * pk, :]
        base_unit(c, 1, u).start()

    def take_edge(i):
        k, c, u = unit(i)
        edge_unit(k, c, u).wait_recv()
        own[k, c, pair(u)] = own[k, c, pair(u)] + from_edge[k, c, pair(u)]
        mid_unit(k, c, u).start()

    def take_mid(i):
        k, c, u = unit(i)
        mid_unit(k, c, u).wait_recv()

        @pl.when(k == 0)
        def _():
            own[Z - 1, c, pair(u)] = own[Z - 1, c, pair(u)] + from_mid[0, c, pair(u)]
            back_unit(c, u).start()

        @pl.when(k == 1)
        def _():
            scatter(c, u, own[Z - 2, c, pair(u)] + from_mid[1, c, pair(u)])

    def take_back(i):
        j = i - U
        c = jnp.where(i < U, 0, jnp.where(i < 3 * U, 1 + lax.rem(j + 2 * U, 2), 3))
        u = jnp.where(i < U, i, jnp.where(i < 3 * U, j // 2, i - 3 * U))
        back_unit(c, u).wait_recv()
        scatter(c, u, own[Z - 1, c, pair(u)] + from_in[c, pair(u)])

    def whole_ebuf(s):
        return pltpu.make_async_remote_copy(
            src_ref=ebuf.at[s], dst_ref=ebuf.at[s], send_sem=last_send, recv_sem=last_recv.at[s],
            device_id={"gx": s}, device_id_type=MESH)

    def whole_base(s):
        return pltpu.make_async_remote_copy(
            src_ref=base.at[s], dst_ref=base.at[s], send_sem=last_send, recv_sem=base_recv.at[s],
            device_id={"gx": s}, device_id_type=MESH)

    near, side, diag = (0,), (1, 2), (3,)
    n_units = 2 * C * U

    def repeat(lo, hi, body):
        def once(t, carry):
            body(t)
            return carry
        lax.fori_loop(lo, hi, once, 0)

    def ready_tile(t):
        load(t).wait()
        split(t)

    pltpu.make_async_copy(gathered.at[g], gathered.at[g], amp_sem).wait()
    for c in small:
        c.wait()
    repeat(first, T, lambda t: load(t).start())
    pl.semaphore_wait(barrier, len(close) + jnp.where(edge, 1, 2))
    spread()
    repeat(0, split_first, ready_tile)
    for h in range(2):
        relay(partner, h).wait_recv()
    prepare(near, near_lhs)

    def tiles(ready):
        def late(t):
            ready_tile(t)
            compute(near, near_lhs, t, ready)

        repeat(0, split_first, lambda t: compute(near, near_lhs, t, ready))
        repeat(split_first, T // 2 + 1, late)
        forward_cross()
        repeat(T // 2 + 1, T - 2, late)
        forward_side()
        repeat(T - 2, T, late)
        arrived(side)
        prepare(side, side_lhs)

    @pl.when(edge)
    def _():
        tiles(((0, 0), (1, 0)))
        repeat(0, T - 3, lambda t: compute(side, side_lhs, t, ((0, 1), (0, 2))))
        forward_diag()
        repeat(T - 3, T, lambda t: compute(side, side_lhs, t, ((0, 1), (0, 2))))
        arrived(diag)
        prepare(diag, far_lhs)
        send_last(g).start()
        repeat(0, T, lambda t: compute(diag, far_lhs, t, ((0, 3),)))

        def rest(u):
            for c in (2, 3):
                edge_unit(1, c, u).start()

        repeat(0, U, lambda u: edge_unit(1, 1, u).start())
        repeat(0, U, rest)
        repeat(0, U, exchange)
        for j in range(1, N):
            s_from = peer(j // 2, j % 2)
            whole_ebuf(s_from).wait_recv()
            send_last(s_from).start()
        repeat(0, n_units // 2, take_back)

    @pl.when(inner)
    def _():
        lag = jnp.where(lower, LAGS[0], LAGS[1])

        def middle(i):
            @pl.when(jnp.logical_and(i >= 0, i < n_units))
            def _():
                take_mid(i)

        def with_side(t):
            compute(side, side_lhs, t)
            take_edge(t)
            middle(t - lag)

        def with_diag(t):
            compute(diag, far_lhs, t)
            take_edge(T + t)
            middle(T + t - lag)

        def both(i):
            take_edge(i)
            middle(i - lag)

        tiles(())
        repeat(0, T - 3, with_side)
        forward_diag()
        repeat(T - 3, T, with_side)
        arrived(diag)
        prepare(diag, far_lhs)
        repeat(0, T, with_diag)
        repeat(2 * T, n_units, both)
        repeat(n_units, n_units + max(LAGS), lambda i: middle(i - lag))

    def put(s):
        band = pl.ds(pl.multiple_of(s * T * W, T * W), T * W)
        return pltpu.make_async_copy(res.at[:, band], res_out.at[:, band], out_sem)

    def finish(s):
        def place(t):
            return pl.ds(pl.multiple_of((s * T + t) * W, W), W)

        @pl.when(edge)
        def _():
            for t in range(T):
                res[:, place(t)] = base[s, t]

        @pl.when(inner)
        def _():
            send_last(s).wait_recv()
            for t in range(T):
                res[:, place(t)] = base[s, t] + last[s, t]

        put(s).start()

    finish(g)

    def collect(j, carry):
        c, i = j // 2, lax.rem(j, 2)
        s = lax.rem(chip // 2 + c // 2, 2) * 2 + lax.rem(lax.rem(chip, 2) + lax.rem(c, 2), 2)
        s = s * 2 + lax.rem(core + i, 2)
        whole_base(s).wait_recv()
        finish(s)
        return carry

    lax.fori_loop(1, N, collect, 0)

    pltpu.make_async_remote_copy(
        src_ref=gathered.at[0:N - 1], dst_ref=gathered.at[0:N - 1], send_sem=ag_send, recv_sem=ag_recv.at[0, 0],
        device_id={"gx": partner}, device_id_type=MESH).wait_send()

    pltpu.make_async_remote_copy(
        src_ref=own.at[0:2], dst_ref=from_edge, send_sem=stream_send, recv_sem=edge_recv.at[0, 0, 0],
        device_id={"row": inward}, device_id_type=MESH).wait_send()

    def sent(ref, sem):
        pltpu.make_async_remote_copy(
            src_ref=ref.at[1:N], dst_ref=ebuf.at[1:N], send_sem=sem, recv_sem=last_recv.at[0],
            device_id={"gx": partner}, device_id_type=MESH).wait_send()

    sent(fin, fin_send)

    @pl.when(edge)
    def _():
        sent(efin, efin_send)
        pltpu.make_async_remote_copy(
            src_ref=ebuf, dst_ref=last, send_sem=last_send, recv_sem=last_recv.at[g],
            device_id={"row": inward}, device_id_type=MESH).wait_send()

    @pl.when(inner)
    def _():
        pltpu.make_async_remote_copy(
            src_ref=own.at[Z - 1], dst_ref=from_in, send_sem=back_send, recv_sem=mid_recv.at[0, 0, 0],
            device_id={"row": outward}, device_id_type=MESH).wait_send()

    pltpu.make_async_copy(res, res_out, out_sem).wait()


def divide(res, pair_occ, occ, energy, res_out, upd_out):
    pk, A = res.shape
    which = lax.broadcasted_iota(jnp.int32, (pk, 1), 0)
    pe = jnp.zeros((pk, 1), jnp.float32)
    for k in range(pk):
        pe = jnp.where(which == k, occ[pair_occ[0, k]] + occ[pair_occ[1, k]], pe)
    v = res[...]
    res_out[...] = v
    upd_out[...] = v / (energy[...] - pe)


def fused_body(N, Z, W, amplitudes, integrals, cd_irrep, ab_irrep, allowed, pair_occ, occ_energy, ab_energy):
    rows, K = amplitudes.shape
    AB = integrals.shape[1]
    A = ab_energy.shape[0]
    T = AB // W
    U = T // 2
    C = N // 2
    pk = rows // Z
    R = 2 * pk
    vmem, smem = pltpu.VMEM, pltpu.SMEM
    f32, bf16, i32 = jnp.float32, jnp.bfloat16, jnp.int32
    dma = pltpu.SemaphoreType.DMA
    out = jax.ShapeDtypeStruct((pk, A), f32)
    residual = pl.pallas_call(
        functools.partial(kernel, N, Z, T, W),
        out_shape=out,
        in_specs=[pl.BlockSpec(memory_space=pltpu.HBM)] * 5,
        out_specs=pl.BlockSpec(memory_space=pltpu.HBM),
        scratch_shapes=[
            smem(cd_irrep.shape, i32), smem(ab_irrep.shape, i32), smem(allowed.shape, i32), dma((3,)), dma,
            vmem((T, K, W), f32), vmem((T, K, W), bf16), vmem((T, K, W), bf16),
            vmem((N, 2, rows // 2, K), f32), vmem((4 * rows, K), f32),
            vmem((4 * rows, K), bf16), vmem((8 * rows, K), bf16), vmem((4 * rows, K), bf16),
            vmem((Z, C, T, R, W), f32), vmem((2, C, T, R, W), f32), vmem((2, C, T, R, W), f32), vmem((C, T, R, W), f32),
            vmem((N, T, pk, W), f32), vmem((N, T, pk, W), f32),
            vmem((N, T, pk, W), f32), vmem((N, T, pk, W), f32), vmem((N, T, pk, W), f32), vmem((pk, A), f32),
            dma((T,)), dma, dma((2, N)), dma, dma((2, C, U)), dma((2, C, U)), dma,
            dma, dma((N,)), dma, dma, dma((N,)), dma,
        ],
        compiler_params=pltpu.CompilerParams(
            collective_id=0, has_side_effects=True, vmem_limit_bytes=VMEM_GRANT),
    )(amplitudes, integrals, cd_irrep, ab_irrep, allowed)
    return pl.pallas_call(
        divide,
        out_shape=(out, out),
        in_specs=[pl.BlockSpec(memory_space=s) for s in (vmem, smem, smem, vmem)],
        out_specs=[pl.BlockSpec(memory_space=vmem)] * 2,
        compiler_params=pltpu.CompilerParams(vmem_limit_bytes=VMEM_GRANT),
    )(residual, pair_occ.T, occ_energy, ab_energy.reshape(1, A))


def solution(mesh):
    N, Z = mesh.shape["gx"], mesh.shape["row"]

    def body(amplitudes, integrals, *rest):
        rows, K = amplitudes.shape
        AB = integrals.shape[1]
        W = 2 * BLK
        pk = rows // Z
        need = 8 * K * AB + 16 * rows * N * K + 16 * rows * N * AB + 28 * pk * AB * N
        if need > VMEM_BUDGET * 3 // 4 or AB % (2 * W) or AB < 6 * W or N != 8 or Z != 4 or rows != 4 * Z:
            return plain_body(amplitudes, integrals, *rest)
        return fused_body(N, Z, W, amplitudes, integrals, *rest)

    return jax.shard_map(
        body,
        mesh=mesh,
        in_specs=(
            P("gx", "row"),
            P("row", "gx"),
            P("row"),
            P("gx"),
            P(),
            P(("gx", "row"), None),
            P(),
            P(),
        ),
        out_specs=(P(("gx", "row"), None), P(("gx", "row"), None)),
        check_vma=False,
    )
```
